32 devices in a mesh: grp: 2 (over x), patch: 16 (over z, y, core).
Axes of the slice: x: 2, y: 2, z: 4, core: 2. Of those that a mesh axis runs over, the one named last changes fastest.
Arguments:
- displace: float32 [2, 32768, 384], P('grp', 'patch'), may hold values from -6 to 6
- velocity: float32 [2, 32768, 384], P('grp', 'patch'), may hold values from -6 to 6
- ext_force: float32 [2, 32768, 384], P('grp', 'patch'), may hold values from -6 to 6
- inv_mass: float32 [2, 32768, 128], P('grp', 'patch'), may hold values from 0.1 to 6
- thickness: float32 [2, 32768, 128], P('grp', 'patch'), may hold values from 0.5 to 2
- stiff_bands: bfloat16 [5, 384, 384], replicated, may hold values from -0.125 to 0.125
- pair_points: int32 [2, 16, 3, 1536], P('grp', 'patch'), may hold values from 0 to 6143
- pair_weights: float32 [2, 16, 3, 1536], P('grp', 'patch'), may hold values from 0.25 to 1
Outputs:
- displace_new: float32 [2, 32768, 384], P('grp', 'patch')
- velocity_new: float32 [2, 32768, 384], P('grp', 'patch')
The draws below stay inside these ranges and needn't reach their ends.
Inputs may be any that keep to these rules, and one draw needn't show every extreme that they name: `pair_points`: entry e names the control point in row e // 3 of the sending block (rows counted within the block) and point e % 3 across the strip.
All inputs are finite; a program needn't handle non-finite values.
Results may differ from the reference program's by a relative error of at most 0.00094.
The reference program's roundings to bfloat16 on the way count: a program that leaves them out, or rounds other values in their place, can miss the bound.
Values may be sent and summed in bfloat16 or wider, within the bound.
A program may use at most 192 MiB of HBM per device.

```python
import math
import jax
import jax.numpy as jnp
from jax import lax

POINTS = 128
REACH = 2
SUBSTEPS = 4
TILES_DEV = 2048
SLOTS = 1536
ROW = 384
EDGE = 3
TILES = 32768
N_PATCH = 16


def draw_inv_mass(key, part):
    key_base, key_block, key_point = jax.random.split(jax.random.fold_in(key, 7), 3)
    block_total = 2 * N_PATCH
    position = jnp.arange(block_total, dtype=jnp.float32) / (block_total - 1)
    jitter = jax.random.uniform(key_block, (block_total,), jnp.float32, -0.05, 0.05)
    start = jax.random.uniform(key_base, (), jnp.float32, math.log(1.2), math.log(1.6))
    ceiling = jnp.exp(start + position * math.log(3.0) + jitter)
    per_row = jnp.repeat(ceiling.reshape(2, N_PATCH), TILES_DEV, axis=1)
    falling = jax.random.uniform(key_point, (2, TILES_DEV * N_PATCH, POINTS), jnp.float32, 0.0, math.log(4.0))
    return (per_row[:, :, None] * jnp.exp(-falling)).astype(jnp.float32)


def set_ends(drawn, rng, low, top_value):
    dims = drawn.shape
    place = [jax.random.randint(jax.random.fold_in(rng, axis), (), 0, dims[axis]) for axis in range(len(dims))]
    drawn = drawn.at[tuple(place)].set(low)
    longest = dims.index(max(dims))
    place[longest] = (place[longest] + 1) % dims[longest]
    return drawn.at[tuple(place)].set(top_value)


def block_scale(own_key, extent, cuts, low, top_value):
    loudness = 1.0
    for dim, shards_of in cuts:
        draws = jax.random.uniform(jax.random.fold_in(jax.random.fold_in(own_key, 6), dim), (shards_of,), jnp.float32, low / len(cuts), top_value / len(cuts))
        loudness = loudness * jnp.repeat(jnp.exp(draws), extent[dim] // shards_of).reshape((-1,) + (1,) * (len(extent) - 1 - dim))
    return loudness


def noise(key, shape, scale, limit, pieces=(), held_as=jnp.bfloat16):
    loudness = block_scale(key, shape, pieces, -0.22, 0.18) if pieces else 1.0
    array = jax.random.normal(key, shape, jnp.float32) * scale * loudness
    return jnp.minimum(jnp.maximum(array, -limit), limit).astype(held_as)


def setup_inputs(seed: int = 0) -> dict:
    seeds = jax.random.split(jax.random.key(seed), 9)
    displace = noise(seeds[0], (2, TILES, ROW), 1.0, 6.0, ((0, 2), (1, 16)), jnp.float32)
    velocity = noise(seeds[1], (2, TILES, ROW), 1.0, 6.0, ((0, 2), (1, 16)), jnp.float32)
    ext_force = noise(seeds[2], (2, TILES, ROW), 1.0, 6.0, ((0, 2), (1, 16)), jnp.float32)
    inv_mass = draw_inv_mass(jax.random.fold_in(seeds[8], 71), 0)
    thickness = jnp.clip(jnp.exp(math.log(2.0) - 1.3862944 * jax.random.uniform(seeds[4], (2, TILES, POINTS), jnp.float32) ** block_scale(seeds[4], (2, TILES, POINTS), ((0, 2), (1, 16)), -0.2, 0.2)), 0.5, 2.0)
    stiff_bands = noise(seeds[5], (2 * REACH + 1, ROW, ROW), ((2 * REACH + 1) * ROW) ** -0.5, 0.125)
    pair_points = set_ends(jax.random.randint(seeds[6], (2, N_PATCH, 3, SLOTS), 0, TILES_DEV * EDGE), jax.random.fold_in(seeds[6], 1), 0, (TILES_DEV * EDGE) - 1).astype(jnp.int32)
    pair_weights = jnp.clip(jnp.exp(math.log(1.0) - 1.3862944 * jax.random.uniform(seeds[7], (2, N_PATCH, 3, SLOTS), jnp.float32) ** block_scale(seeds[7], (2, N_PATCH, 3, SLOTS), ((0, 2), (1, 16)), -0.2, 0.2)), 0.25, 1.0)
    return dict(displace=displace, velocity=velocity, ext_force=ext_force, inv_mass=inv_mass, thickness=thickness, stiff_bands=stiff_bands, pair_points=pair_points, pair_weights=pair_weights)


PENALTY = 1.0
DAMPING = 0.5
COURANT = 0.4

def band_force(field, thickness, stiff_bands):
    row_count = field.shape[0]
    operand = lax.optimization_barrier(field.astype(jnp.bfloat16)).astype(jnp.float32)
    padded = jnp.pad(operand, ((REACH, REACH), (0, 0)))
    summed = jnp.zeros((row_count, 3 * POINTS), jnp.float32)
    for band_index in range(2 * REACH + 1):
        summed = summed + jnp.dot(padded[band_index:band_index + row_count], stiff_bands[band_index].astype(jnp.float32), precision=lax.Precision.HIGHEST)
    return (summed.reshape(row_count, 3, POINTS) * thickness[:, None, :]).reshape(row_count, 3 * POINTS)

def reference(displace, velocity, ext_force, inv_mass, thickness, stiff_bands, pair_points, pair_weights):
    row_width = 3 * POINTS
    base_step = COURANT * jnp.min(1.0 / jnp.sqrt(inv_mass * thickness))
    forces = [band_force(displace[group_index], thickness[group_index], stiff_bands) for group_index in range(2)]
    patch_base = (jnp.arange(N_PATCH, dtype=jnp.int32) * (TILES_DEV * row_width))[:, None, None]
    comp_offset = (jnp.arange(3, dtype=jnp.int32) * POINTS)[:, None, None, None]
    traces = []
    indices = []
    for group_index in range(2):
        pair_table = pair_points[group_index]
        flat_index = patch_base + pair_table // EDGE * row_width + pair_table % EDGE
        flat_index = (flat_index[None] + comp_offset).astype(jnp.int32)
        gathered = jnp.stack([displace[group_index].reshape(-1)[flat_index], velocity[group_index].reshape(-1)[flat_index], forces[group_index].reshape(-1)[flat_index]])
        traces.append(gathered)
        indices.append(flat_index)
    neighbour = (jnp.arange(N_PATCH, dtype=jnp.int32)[:, None] + jnp.arange(3, dtype=jnp.int32)[None, :] - 1).astype(jnp.int32)
    present = ((neighbour >= 0) & (neighbour < N_PATCH)).astype(jnp.float32)
    clipped = jnp.clip(neighbour, 0, N_PATCH - 1).astype(jnp.int32)
    mirror = jnp.broadcast_to((2 - jnp.arange(3, dtype=jnp.int32))[None, :], (N_PATCH, 3)).astype(jnp.int32)
    results_disp = []
    results_vel = []
    for group_index in range(2):
        gathered = traces[group_index]
        partner = traces[1 - group_index][:, :, clipped, mirror, :]
        weight = pair_weights[group_index] * present[:, :, None]
        slot_force = weight[None] * (-PENALTY * (gathered[0] - partner[0]) - DAMPING * (gathered[1] - partner[1]) + 0.5 * (partner[2] - gathered[2]))
        coupling = jnp.zeros((TILES * row_width,), jnp.float32).at[indices[group_index].reshape(-1)].add(slot_force.reshape(-1)).reshape(TILES, row_width)
        field = displace[group_index]
        moving = velocity[group_index]
        if group_index == 0:
            step_count = 1
            step_size = SUBSTEPS * base_step
        else:
            step_count = SUBSTEPS
            step_size = base_step
        for substep in range(step_count):
            if substep == 0:
                inner_force = forces[group_index]
            else:
                inner_force = band_force(field, thickness[group_index], stiff_bands)
            accel_now = ((ext_force[group_index] + coupling - inner_force).reshape(TILES, 3, POINTS) * inv_mass[group_index][:, None, :]).reshape(TILES, row_width)
            moving = moving + step_size * accel_now
            field = field + step_size * moving
        results_disp.append(field)
        results_vel.append(moving)
    return (jnp.stack(results_disp), jnp.stack(results_vel))
```

```python
import functools

import jax
import jax.numpy as jnp
from jax import lax
from jax.experimental import pallas as pl
from jax.experimental.pallas import tpu as pltpu
from jax.sharding import PartitionSpec as P

POINTS = 128
REACH = 2
SUBSTEPS = 4
EDGE = 3
COURANT = 0.4
HALO = REACH * SUBSTEPS
BASE = 2 * HALO
LANES = 128
MESH = pl.DeviceIdType.MESH


def row_chunk(rows, most):
    tiles = rows // 8
    return 8 * max(d for d in range(1, tiles + 1) if tiles % d == 0 and 8 * d <= most)


def iota(shape, dim):
    return lax.broadcasted_iota(jnp.int32, shape, dim)


def kernel(
    n_grp,
    n_patch,
    disp_hbm,
    vel_hbm,
    ext_hbm,
    mass_hbm,
    thick_hbm,
    band_hbm,
    pts_ref,
    wts_ref,
    disp_out,
    vel_out,
    xa,
    xb,
    vel,
    frc,
    ext,
    mass,
    thick,
    band,
    table,
    sent,
    got,
    spread,
    peak,
    load_sem,
    halo_send,
    halo_recv,
    trace_send,
    trace_recv,
    far_send,
    far_recv,
    peak_send,
    peak_recv,
    out_sem,
):
    g = lax.axis_index("grp")
    p = lax.axis_index("patch")
    rows = disp_hbm.shape[1]
    width = disp_hbm.shape[2]
    slots = pts_ref.shape[3]
    total = rows + 2 * BASE
    own = pl.ds(BASE, rows)
    has_low = p > 0
    has_high = p < n_patch - 1

    loads = [
        pltpu.make_async_copy(mass_hbm.at[0], mass.at[own], load_sem.at[0]),
        pltpu.make_async_copy(thick_hbm.at[0], thick.at[own], load_sem.at[1]),
        pltpu.make_async_copy(band_hbm, band, load_sem.at[2]),
        pltpu.make_async_copy(disp_hbm.at[0], xa.at[own], load_sem.at[3]),
        pltpu.make_async_copy(vel_hbm.at[0], vel.at[own], load_sem.at[4]),
        pltpu.make_async_copy(ext_hbm.at[0], ext.at[own], load_sem.at[5]),
    ]
    for load in loads:
        load.start()

    def halo_copy(k, up):
        source, target = ((disp_hbm, xa), (vel_hbm, vel), (mass_hbm, mass), (thick_hbm, thick))[k]
        if up:
            src = source.at[0, pl.ds(rows - HALO, HALO)]
            dst = target.at[pl.ds(BASE - HALO, HALO)]
            to = p + 1
        else:
            src = source.at[0, pl.ds(0, HALO)]
            dst = target.at[pl.ds(BASE + rows, HALO)]
            to = p - 1
        return pltpu.make_async_remote_copy(
            src_ref=src,
            dst_ref=dst,
            send_sem=halo_send.at[k, int(up)],
            recv_sem=halo_recv.at[k, int(up)],
            device_id={"grp": g, "patch": to},
            device_id_type=MESH,
        )

    @pl.when(has_high)
    def _():
        for k in range(4):
            halo_copy(k, True).start()

    @pl.when(has_low)
    def _():
        for k in range(4):
            halo_copy(k, False).start()

    for buf in (xa, xb, vel, frc, ext, mass, thick):
        zero = jnp.zeros((HALO, buf.shape[1]), jnp.float32)
        buf[pl.ds(0, HALO), :] = zero
        buf[pl.ds(total - HALO, HALO), :] = zero

    @pl.when(p == 0)
    def _():
        for buf in (xa, vel, ext, mass, thick):
            buf[pl.ds(BASE - HALO, HALO), :] = jnp.zeros((HALO, buf.shape[1]), jnp.float32)
        got[0] = jnp.zeros(got.shape[1:], jnp.float32)

    @pl.when(p == n_patch - 1)
    def _():
        for buf in (xa, vel, ext, mass, thick):
            buf[pl.ds(BASE + rows, HALO), :] = jnp.zeros((HALO, buf.shape[1]), jnp.float32)
        got[2] = jnp.zeros(got.shape[1:], jnp.float32)

    loads[0].wait()
    loads[1].wait()
    peak_rows = row_chunk(rows, 256)

    def peak_step(i, high):
        at = pl.ds(pl.multiple_of(BASE + i * peak_rows, 8), peak_rows)
        product = (mass[at, :] * thick[at, :]).reshape(peak_rows // 8, 8, LANES)
        return jnp.maximum(high, jnp.max(product, axis=0))

    peak[0] = lax.fori_loop(
        0, rows // peak_rows, peak_step, jnp.zeros((8, LANES), jnp.float32)
    )
    count = n_grp * n_patch
    me = g * n_patch + p

    def peak_start(k, carry):
        to = (me + k) % count
        pltpu.make_async_remote_copy(
            src_ref=peak.at[0],
            dst_ref=peak.at[k],
            send_sem=peak_send,
            recv_sem=peak_recv,
            device_id={"grp": to // n_patch, "patch": to % n_patch},
            device_id_type=MESH,
        ).start()
        return carry

    lax.fori_loop(1, count, peak_start, 0)

    def force(src, at, length):
        around = src[pl.ds(pl.multiple_of(at - 8, 8), length + 16), :]
        parts = [
            around[8 + b - REACH : 8 + b - REACH + length].astype(jnp.bfloat16)
            for b in range(2 * REACH + 1)
        ]
        summed = jnp.dot(
            jnp.concatenate(parts, axis=1), band[...], preferred_element_type=jnp.float32
        )
        t = thick[pl.ds(at, length), :]
        return summed * jnp.concatenate([t, t, t], axis=1)

    loads[2].wait()
    loads[3].wait()

    @pl.when(has_low)
    def _():
        for k in range(4):
            halo_copy(k, True).wait_recv()

    @pl.when(has_high)
    def _():
        for k in range(4):
            halo_copy(k, False).wait_recv()

    wide_chunk = row_chunk(rows + 2 * HALO, 352)
    wide_count = (rows + 2 * HALO) // wide_chunk

    def first_force(i, carry):
        at = pl.multiple_of(HALO + i * wide_chunk, 8)
        frc[pl.ds(at, wide_chunk), :] = force(xa, at, wide_chunk)
        return carry

    lax.fori_loop(0, wide_count, first_force, 0)
    loads[4].wait()

    blocks = rows // LANES

    def edge_mix(at, length):
        return xa[pl.ds(at, length), :] + 0.5 * (
            vel[pl.ds(at, length), :] + frc[pl.ds(at, length), :]
        )

    key = iota((16, width), 0)
    lane = iota((16, width), 1)
    pick = jnp.where(
        (key % 4 == lane // POINTS) & (key // 4 == lane % POINTS), 1.0, 0.0
    ).astype(jnp.bfloat16)

    def table_step(h, carry):
        at = pl.multiple_of(BASE + h * LANES, 8)
        mix = edge_mix(at, LANES).astype(jnp.bfloat16)
        table[pl.ds(pl.multiple_of(h * 16, 16), 16), :] = lax.dot_general(
            pick, mix, (((1,), (1,)), ((), ())), preferred_element_type=jnp.float32
        ).astype(jnp.bfloat16)
        return carry

    lax.fori_loop(0, blocks, table_step, 0)

    slot_chunk = min(512, slots)
    slot_count = slots // slot_chunk
    key_col = iota((16, slot_chunk), 0) // 4
    low_col = iota((LANES, slot_chunk), 0)
    out_row = iota((8, 16), 0) % 4
    in_key = iota((8, 16), 1)
    fold = jnp.where((in_key % 4 == out_row) & (out_row < 3), 1.0, 0.0).astype(jnp.bfloat16)

    def slot_split(j, at):
        entry = pts_ref[0, 0, pl.ds(j, 1), at]
        row = entry // EDGE
        return row // LANES, row % LANES, entry - row * EDGE

    def trace_copy(j):
        return pltpu.make_async_remote_copy(
            src_ref=sent.at[j],
            dst_ref=got.at[2 - j],
            send_sem=trace_send.at[j],
            recv_sem=trace_recv.at[2 - j],
            device_id={"grp": 1 - g, "patch": p + (j - 1)},
            device_id_type=MESH,
        )

    exists = (has_low, None, has_high)

    def guarded(cond, run):
        if cond is None:
            run()
        else:
            pl.when(cond)(run)

    for j in range(3):

        def gather_step(c, carry, j=j):
            at = pl.ds(pl.multiple_of(c * slot_chunk, LANES), slot_chunk)
            high, low, point = slot_split(j, at)
            hot = jnp.where(low_col == low, 1.0, 0.0).astype(jnp.bfloat16)
            found = jnp.dot(table[...], hot, preferred_element_type=jnp.float32)
            total_found = jnp.zeros((16, slot_chunk), jnp.float32)
            for h in range(blocks):
                total_found = jnp.where(high == h, found[h * 16 : h * 16 + 16], total_found)
            total_found = jnp.where(key_col == point, total_found, 0.0)
            sent[j, :, at] = jnp.dot(
                fold, total_found.astype(jnp.bfloat16), preferred_element_type=jnp.float32
            )
            return carry

        lax.fori_loop(0, slot_count, gather_step, 0)
        guarded(exists[j], lambda j=j: trace_copy(j).start())

    spread[...] = jnp.zeros(spread.shape, jnp.float32)
    one_row = jnp.where(iota((8, slot_chunk), 0) % 4 == 3, 1.0, 0.0)
    for j in (1, 0, 2):
        guarded(exists[j], lambda j=j: trace_copy(2 - j).wait_recv())
        present = 1.0 if exists[j] is None else jnp.where(exists[j], 1.0, 0.0)

        def spread_step(c, carry, j=j, present=present):
            at = pl.ds(pl.multiple_of(c * slot_chunk, LANES), slot_chunk)
            high, low, point = slot_split(j, at)
            weight = wts_ref[0, 0, pl.ds(j, 1), at] * present
            value = (got[j, :, at] + one_row) * weight
            value = jnp.where(key_col == point, jnp.concatenate([value, value], axis=0), 0.0)
            coarse = value.astype(jnp.bfloat16).astype(jnp.float32)
            fine = value - coarse
            pieces = [jnp.where(high == h, coarse, 0.0).astype(jnp.bfloat16) for h in range(blocks)]
            pieces += [jnp.where(high == h, fine, 0.0).astype(jnp.bfloat16) for h in range(blocks)]
            hot = jnp.where(low_col == low, 1.0, 0.0).astype(jnp.bfloat16)
            spread[...] += lax.dot_general(
                jnp.concatenate(pieces, axis=0),
                hot,
                (((1,), (1,)), ((), ())),
                preferred_element_type=jnp.float32,
            )
            return carry

        lax.fori_loop(0, slot_count, spread_step, 0)

    loads[5].wait()
    key2 = iota((LANES, 2 * width), 0)
    lane2 = iota((LANES, 2 * width), 1)
    place_key = key2 % 16
    comp = place_key % 4
    hit = comp == jnp.where(lane2 < width, lane2 // POINTS, 3)
    place = jnp.where(
        hit & (place_key // 4 == lane2 % POINTS) & (key2 < 48), 1.0, 0.0
    ).astype(jnp.bfloat16)

    def couple_step(i, carry):
        h = (i + blocks - 1) % blocks
        summed = (
            spread[pl.ds(pl.multiple_of(h * 16, 16), 16), :]
            + spread[pl.ds(pl.multiple_of((blocks + h) * 16, 16), 16), :]
        )
        first = summed.astype(jnp.bfloat16).astype(jnp.float32)
        rest = summed - first
        second = rest.astype(jnp.bfloat16).astype(jnp.float32)
        stack = jnp.concatenate(
            [first, second, rest - second, jnp.zeros((LANES - 48, LANES), jnp.float32)], axis=0
        )
        placed = jnp.dot(
            stack.T.astype(jnp.bfloat16), place, preferred_element_type=jnp.float32
        )
        at = pl.multiple_of(BASE + h * LANES, 8)
        mix = edge_mix(at, LANES)
        ext[pl.ds(at, LANES), :] += placed[:, :width] - mix * placed[:, width:]
        return carry

    def far_copy(up):
        if up:
            src, dst, to = pl.ds(BASE + rows - HALO, HALO), pl.ds(BASE - HALO, HALO), p + 1
        else:
            src, dst, to = pl.ds(BASE, HALO), pl.ds(BASE + rows, HALO), p - 1
        return pltpu.make_async_remote_copy(
            src_ref=ext.at[src],
            dst_ref=ext.at[dst],
            send_sem=far_send.at[int(up)],
            recv_sem=far_recv.at[int(up)],
            device_id={"grp": g, "patch": to},
            device_id_type=MESH,
        )

    fine_group = g == 1
    lax.fori_loop(0, 2, couple_step, 0)
    pl.when(fine_group & has_high)(lambda: far_copy(True).start())
    pl.when(fine_group & has_low)(lambda: far_copy(False).start())
    lax.fori_loop(2, blocks, couple_step, 0)

    arrived = peak.at[pl.ds(1, count - 1)]
    pltpu.make_async_copy(arrived, arrived, peak_recv).wait()
    top = jnp.max(jnp.max(peak[...], axis=0), axis=(0, 1), keepdims=True)
    base_step = COURANT * (1.0 / jnp.sqrt(top))
    size = jnp.where(g == 0, SUBSTEPS * base_step, base_step)

    pl.when(fine_group & has_low)(lambda: far_copy(True).wait_recv())
    pl.when(fine_group & has_high)(lambda: far_copy(False).wait_recv())

    def advance(src, dst, at, length, inner):
        m = mass[pl.ds(at, length), :]
        moved = vel[pl.ds(at, length), :] + size * (
            jnp.concatenate([m, m, m], axis=1) * (ext[pl.ds(at, length), :] - inner)
        )
        vel[pl.ds(at, length), :] = moved
        dst[pl.ds(at, length), :] = src[pl.ds(at, length), :] + size * moved

    plain_chunk = row_chunk(rows, 256)
    plain_count = rows // plain_chunk

    def outputs(src, i):
        at = pl.multiple_of(i * plain_chunk, 8)
        here = pl.ds(BASE + at, plain_chunk)
        there = pl.ds(at, plain_chunk)
        return (
            pltpu.make_async_copy(src.at[here], disp_out.at[0, there], out_sem.at[0, i]),
            pltpu.make_async_copy(vel.at[here], vel_out.at[0, there], out_sem.at[1, i]),
        )

    def put(src, i):
        for copy in outputs(src, i):
            copy.start()

    @pl.when(g == 0)
    def _():
        def step(i, carry):
            at = pl.multiple_of(BASE + i * plain_chunk, 8)
            advance(xa, xb, at, plain_chunk, frc[pl.ds(at, plain_chunk), :])
            put(xb, i)
            return carry

        lax.fori_loop(0, plain_count, step, 0)

    @pl.when(fine_group)
    def _():
        def step(i, carry):
            at = pl.multiple_of(HALO + i * wide_chunk, 8)
            advance(xa, xb, at, wide_chunk, frc[pl.ds(at, wide_chunk), :])
            return carry

        lax.fori_loop(0, wide_count, step, 0)
        src, dst = xb, xa
        for _ in range(SUBSTEPS - 2):

            def step(i, carry, src=src, dst=dst):
                at = pl.multiple_of(HALO + i * wide_chunk, 8)
                advance(src, dst, at, wide_chunk, force(src, at, wide_chunk))
                return carry

            lax.fori_loop(0, wide_count, step, 0)
            src, dst = dst, src

        def step(i, carry):
            at = pl.multiple_of(BASE + i * plain_chunk, 8)
            advance(src, dst, at, plain_chunk, force(src, at, plain_chunk))
            put(dst, i)
            return carry

        lax.fori_loop(0, plain_count, step, 0)

    last = (xb, xa)[(SUBSTEPS - 1) % 2]

    def drain(src):
        def step(i, carry):
            for copy in outputs(src, i):
                copy.wait()
            return carry

        lax.fori_loop(0, plain_count, step, 0)

    pl.when(g == 0)(lambda: drain(xb))
    pl.when(fine_group)(lambda: drain(last))

    @pl.when(has_high)
    def _():
        for k in range(4):
            halo_copy(k, True).wait_send()

    @pl.when(has_low)
    def _():
        for k in range(4):
            halo_copy(k, False).wait_send()

    for j in range(3):
        guarded(exists[j], lambda j=j: trace_copy(j).wait_send())
    pl.when(fine_group & has_high)(lambda: far_copy(True).wait_send())
    pl.when(fine_group & has_low)(lambda: far_copy(False).wait_send())
    pltpu.make_async_copy(arrived, arrived, peak_send).wait()


def per_device(
    n_grp,
    n_patch,
    displace,
    velocity,
    ext_force,
    inv_mass,
    thickness,
    stiff_bands,
    pair_points,
    pair_weights,
):
    rows, width = displace.shape[1:]
    slots = pair_points.shape[3]
    total = rows + 2 * BASE
    blocks = rows // LANES
    bands = stiff_bands.reshape(stiff_bands.shape[0] * width, width)
    anywhere = pl.BlockSpec(memory_space=pl.ANY)
    vmem = pl.BlockSpec(memory_space=pltpu.VMEM)
    wide = pltpu.VMEM((total, width), jnp.float32)
    slim = pltpu.VMEM((total, POINTS), jnp.float32)
    dma = pltpu.SemaphoreType.DMA
    plain_count = rows // row_chunk(rows, 256)
    return pl.pallas_call(
        functools.partial(kernel, n_grp, n_patch),
        out_shape=[jax.ShapeDtypeStruct(displace.shape, jnp.float32)] * 2,
        in_specs=[anywhere] * 6 + [vmem] * 2,
        out_specs=[anywhere] * 2,
        scratch_shapes=[
            wide,
            wide,
            wide,
            wide,
            wide,
            slim,
            slim,
            pltpu.VMEM(bands.shape, jnp.bfloat16),
            pltpu.VMEM((blocks * 16, LANES), jnp.bfloat16),
            pltpu.VMEM((3, 8, slots), jnp.float32),
            pltpu.VMEM((3, 8, slots), jnp.float32),
            pltpu.VMEM((blocks * 32, LANES), jnp.float32),
            pltpu.VMEM((n_grp * n_patch, 8, LANES), jnp.float32),
            dma((6,)),
            dma((4, 2)),
            dma((4, 2)),
            dma((3,)),
            dma((3,)),
            dma((2,)),
            dma((2,)),
            dma,
            dma,
            dma((2, plain_count)),
        ],
        compiler_params=pltpu.CompilerParams(
            has_side_effects=True, vmem_limit_bytes=56 * 1024 * 1024
        ),
        name="shell_step",
    )(displace, velocity, ext_force, inv_mass, thickness, bands, pair_points, pair_weights)


def solution(mesh):
    return jax.shard_map(
        functools.partial(per_device, mesh.shape["grp"], mesh.shape["patch"]),
        mesh=mesh,
        in_specs=(
            P("grp", "patch", None),
            P("grp", "patch", None),
            P("grp", "patch", None),
            P("grp", "patch", None),
            P("grp", "patch", None),
            P(),
            P("grp", "patch", None, None),
            P("grp", "patch", None, None),
        ),
        out_specs=(P("grp", "patch", None), P("grp", "patch", None)),
        check_vma=False,
    )
```

```python
import functools

import jax
import jax.numpy as jnp
from jax import lax
from jax.experimental import pallas as pl
from jax.experimental.pallas import tpu as pltpu
from jax.sharding import PartitionSpec as P

POINTS = 128
REACH = 2
SUBSTEPS = 4
EDGE = 3
COURANT = 0.4
HALO = REACH * SUBSTEPS
BASE = 2 * HALO
LANES = 128
MESH = pl.DeviceIdType.MESH


def row_chunk(rows, most):
    tiles = rows // 8
    return 8 * max(d for d in range(1, tiles + 1) if tiles % d == 0 and 8 * d <= most)


def iota(shape, dim):
    return lax.broadcasted_iota(jnp.int32, shape, dim)


def force(src, band, thick, at, length):
    around = src[pl.ds(pl.multiple_of(at - 8, 8), length + 16), :]
    parts = [
        around[8 + b - REACH : 8 + b - REACH + length].astype(jnp.bfloat16)
        for b in range(2 * REACH + 1)
    ]
    summed = jnp.dot(
        jnp.concatenate(parts, axis=1), band[...], preferred_element_type=jnp.float32
    )
    t = thick[pl.ds(at, length), :]
    return summed * jnp.concatenate([t, t, t], axis=1)


def advance(size, src, dst, vel, vel_dst, ext, mass, at, length, inner):
    m = mass[pl.ds(at, length), :]
    moved = vel[pl.ds(at, length), :] + size * (
        jnp.concatenate([m, m, m], axis=1) * (ext[pl.ds(at, length), :] - inner)
    )
    vel_dst[pl.ds(at, length), :] = moved
    dst[pl.ds(at, length), :] = src[pl.ds(at, length), :] + size * moved


def kernel(
    n_grp,
    n_patch,
    disp_hbm,
    vel_hbm,
    ext_hbm,
    mass_hbm,
    thick_hbm,
    band_hbm,
    pts_ref,
    wts_ref,
    xb,
    vel,
    ext,
    mass,
    thick,
    size_out,
    xa,
    frc,
    band,
    table,
    sent,
    got,
    spread,
    peak,
    load_sem,
    halo_send,
    halo_recv,
    trace_send,
    trace_recv,
    far_send,
    far_recv,
    peak_send,
    peak_recv,
):
    g = lax.axis_index("grp")
    p = lax.axis_index("patch")
    rows = disp_hbm.shape[1]
    width = disp_hbm.shape[2]
    slots = pts_ref.shape[2]
    total = rows + 2 * BASE
    own = pl.ds(BASE, rows)
    has_low = p > 0
    has_high = p < n_patch - 1

    loads = [
        pltpu.make_async_copy(mass_hbm.at[0], mass.at[own], load_sem.at[0]),
        pltpu.make_async_copy(thick_hbm.at[0], thick.at[own], load_sem.at[1]),
        pltpu.make_async_copy(band_hbm, band, load_sem.at[2]),
        pltpu.make_async_copy(disp_hbm.at[0], xa.at[own], load_sem.at[3]),
        pltpu.make_async_copy(vel_hbm.at[0], vel.at[own], load_sem.at[4]),
        pltpu.make_async_copy(ext_hbm.at[0], ext.at[own], load_sem.at[5]),
    ]
    for load in loads:
        load.start()

    def halo_copy(k, up):
        source, target = ((disp_hbm, xa), (vel_hbm, vel), (mass_hbm, mass), (thick_hbm, thick))[k]
        if up:
            src = source.at[0, pl.ds(rows - HALO, HALO)]
            dst = target.at[pl.ds(BASE - HALO, HALO)]
            to = p + 1
        else:
            src = source.at[0, pl.ds(0, HALO)]
            dst = target.at[pl.ds(BASE + rows, HALO)]
            to = p - 1
        return pltpu.make_async_remote_copy(
            src_ref=src,
            dst_ref=dst,
            send_sem=halo_send.at[k, int(up)],
            recv_sem=halo_recv.at[k, int(up)],
            device_id={"grp": g, "patch": to},
            device_id_type=MESH,
        )

    @pl.when(has_high)
    def _():
        for k in range(4):
            halo_copy(k, True).start()

    @pl.when(has_low)
    def _():
        for k in range(4):
            halo_copy(k, False).start()

    for buf in (xa, xb, vel, frc, ext, mass, thick):
        zero = jnp.zeros((HALO, buf.shape[1]), jnp.float32)
        buf[pl.ds(0, HALO), :] = zero
        buf[pl.ds(total - HALO, HALO), :] = zero

    @pl.when(p == 0)
    def _():
        for buf in (xa, vel, ext, mass, thick):
            buf[pl.ds(BASE - HALO, HALO), :] = jnp.zeros((HALO, buf.shape[1]), jnp.float32)
        got[0] = jnp.zeros(got.shape[1:], jnp.float32)

    @pl.when(p == n_patch - 1)
    def _():
        for buf in (xa, vel, ext, mass, thick):
            buf[pl.ds(BASE + rows, HALO), :] = jnp.zeros((HALO, buf.shape[1]), jnp.float32)
        got[2] = jnp.zeros(got.shape[1:], jnp.float32)

    loads[0].wait()
    loads[1].wait()
    peak_rows = row_chunk(rows, 256)

    def peak_step(i, high):
        at = pl.ds(pl.multiple_of(BASE + i * peak_rows, 8), peak_rows)
        product = (mass[at, :] * thick[at, :]).reshape(peak_rows // 8, 8, LANES)
        return jnp.maximum(high, jnp.max(product, axis=0))

    peak[0] = lax.fori_loop(
        0, rows // peak_rows, peak_step, jnp.zeros((8, LANES), jnp.float32)
    )
    count = n_grp * n_patch
    me = g * n_patch + p

    def peak_start(k, carry):
        to = (me + k) % count
        pltpu.make_async_remote_copy(
            src_ref=peak.at[0],
            dst_ref=peak.at[k],
            send_sem=peak_send,
            recv_sem=peak_recv,
            device_id={"grp": to // n_patch, "patch": to % n_patch},
            device_id_type=MESH,
        ).start()
        return carry

    lax.fori_loop(1, count, peak_start, 0)

    loads[2].wait()
    loads[3].wait()

    @pl.when(has_low)
    def _():
        for k in range(4):
            halo_copy(k, True).wait_recv()

    @pl.when(has_high)
    def _():
        for k in range(4):
            halo_copy(k, False).wait_recv()

    wide_chunk = row_chunk(rows + 2 * HALO, 352)
    wide_count = (rows + 2 * HALO) // wide_chunk

    def first_force(i, carry):
        at = pl.multiple_of(HALO + i * wide_chunk, 8)
        frc[pl.ds(at, wide_chunk), :] = force(xa, band, thick, at, wide_chunk)
        return carry

    lax.fori_loop(0, wide_count, first_force, 0)
    loads[4].wait()

    blocks = rows // LANES

    def edge_mix(at, length):
        return xa[pl.ds(at, length), :] + 0.5 * (
            vel[pl.ds(at, length), :] + frc[pl.ds(at, length), :]
        )

    key = iota((16, width), 0)
    lane = iota((16, width), 1)
    pick = jnp.where(
        (key % 4 == lane // POINTS) & (key // 4 == lane % POINTS), 1.0, 0.0
    ).astype(jnp.bfloat16)

    def table_step(h, carry):
        at = pl.multiple_of(BASE + h * LANES, 8)
        mix = edge_mix(at, LANES).astype(jnp.bfloat16)
        table[pl.ds(pl.multiple_of(h * 16, 16), 16), :] = lax.dot_general(
            pick, mix, (((1,), (1,)), ((), ())), preferred_element_type=jnp.float32
        ).astype(jnp.bfloat16)
        return carry

    lax.fori_loop(0, blocks, table_step, 0)

    slot_chunk = min(512, slots)
    slot_count = slots // slot_chunk
    key_col = iota((16, slot_chunk), 0) // 4
    low_col = iota((LANES, slot_chunk), 0)
    out_row = iota((8, 16), 0) % 4
    in_key = iota((8, 16), 1)
    fold = jnp.where((in_key % 4 == out_row) & (out_row < 3), 1.0, 0.0).astype(jnp.bfloat16)

    def slot_split(j, at):
        entry = pts_ref[j, :, at]
        row = entry // EDGE
        return row // LANES, row % LANES, entry - row * EDGE

    def trace_copy(j):
        return pltpu.make_async_remote_copy(
            src_ref=sent.at[j],
            dst_ref=got.at[2 - j],
            send_sem=trace_send.at[j],
            recv_sem=trace_recv.at[2 - j],
            device_id={"grp": 1 - g, "patch": p + (j - 1)},
            device_id_type=MESH,
        )

    exists = (has_low, None, has_high)

    def guarded(cond, run):
        if cond is None:
            run()
        else:
            pl.when(cond)(run)

    for j in range(3):

        def gather_step(c, carry, j=j):
            at = pl.ds(pl.multiple_of(c * slot_chunk, LANES), slot_chunk)
            high, low, point = slot_split(j, at)
            hot = jnp.where(low_col == low, 1.0, 0.0).astype(jnp.bfloat16)
            found = jnp.dot(table[...], hot, preferred_element_type=jnp.float32)
            total_found = jnp.zeros((16, slot_chunk), jnp.float32)
            for h in range(blocks):
                total_found = jnp.where(high == h, found[h * 16 : h * 16 + 16], total_found)
            total_found = jnp.where(key_col == point, total_found, 0.0)
            sent[j, :, at] = jnp.dot(
                fold, total_found.astype(jnp.bfloat16), preferred_element_type=jnp.float32
            )
            return carry

        lax.fori_loop(0, slot_count, gather_step, 0)
        guarded(exists[j], lambda j=j: trace_copy(j).start())

    spread[...] = jnp.zeros(spread.shape, jnp.float32)
    one_row = jnp.where(iota((8, slot_chunk), 0) % 4 == 3, 1.0, 0.0)
    for j in (1, 0, 2):
        guarded(exists[j], lambda j=j: trace_copy(2 - j).wait_recv())
        present = 1.0 if exists[j] is None else jnp.where(exists[j], 1.0, 0.0)

        def spread_step(c, carry, j=j, present=present):
            at = pl.ds(pl.multiple_of(c * slot_chunk, LANES), slot_chunk)
            high, low, point = slot_split(j, at)
            weight = wts_ref[j, :, at] * present
            value = (got[j, :, at] + one_row) * weight
            value = jnp.where(key_col == point, jnp.concatenate([value, value], axis=0), 0.0)
            coarse = value.astype(jnp.bfloat16).astype(jnp.float32)
            fine = value - coarse
            pieces = [jnp.where(high == h, coarse, 0.0).astype(jnp.bfloat16) for h in range(blocks)]
            pieces += [jnp.where(high == h, fine, 0.0).astype(jnp.bfloat16) for h in range(blocks)]
            hot = jnp.where(low_col == low, 1.0, 0.0).astype(jnp.bfloat16)
            spread[...] += lax.dot_general(
                jnp.concatenate(pieces, axis=0),
                hot,
                (((1,), (1,)), ((), ())),
                preferred_element_type=jnp.float32,
            )
            return carry

        lax.fori_loop(0, slot_count, spread_step, 0)

    loads[5].wait()
    key2 = iota((LANES, 2 * width), 0)
    lane2 = iota((LANES, 2 * width), 1)
    place_key = key2 % 16
    comp = place_key % 4
    hit = comp == jnp.where(lane2 < width, lane2 // POINTS, 3)
    place = jnp.where(
        hit & (place_key // 4 == lane2 % POINTS) & (key2 < 48), 1.0, 0.0
    ).astype(jnp.bfloat16)

    def couple_step(i, carry):
        h = (i + blocks - 1) % blocks
        summed = (
            spread[pl.ds(pl.multiple_of(h * 16, 16), 16), :]
            + spread[pl.ds(pl.multiple_of((blocks + h) * 16, 16), 16), :]
        )
        first = summed.astype(jnp.bfloat16).astype(jnp.float32)
        rest = summed - first
        second = rest.astype(jnp.bfloat16).astype(jnp.float32)
        stack = jnp.concatenate(
            [first, second, rest - second, jnp.zeros((LANES - 48, LANES), jnp.float32)], axis=0
        )
        placed = jnp.dot(
            stack.T.astype(jnp.bfloat16), place, preferred_element_type=jnp.float32
        )
        at = pl.multiple_of(BASE + h * LANES, 8)
        mix = edge_mix(at, LANES)
        ext[pl.ds(at, LANES), :] += placed[:, :width] - mix * placed[:, width:]
        return carry

    def far_copy(up):
        if up:
            src, dst, to = pl.ds(BASE + rows - HALO, HALO), pl.ds(BASE - HALO, HALO), p + 1
        else:
            src, dst, to = pl.ds(BASE, HALO), pl.ds(BASE + rows, HALO), p - 1
        return pltpu.make_async_remote_copy(
            src_ref=ext.at[src],
            dst_ref=ext.at[dst],
            send_sem=far_send.at[int(up)],
            recv_sem=far_recv.at[int(up)],
            device_id={"grp": g, "patch": to},
            device_id_type=MESH,
        )

    fine_group = g == 1
    lax.fori_loop(0, 2, couple_step, 0)
    pl.when(fine_group & has_high)(lambda: far_copy(True).start())
    pl.when(fine_group & has_low)(lambda: far_copy(False).start())
    lax.fori_loop(2, blocks, couple_step, 0)

    arrived = peak.at[pl.ds(1, count - 1)]
    pltpu.make_async_copy(arrived, arrived, peak_recv).wait()
    top = jnp.max(jnp.max(peak[...], axis=0), axis=(0, 1), keepdims=True)
    base_step = COURANT * (1.0 / jnp.sqrt(top))
    size = jnp.where(g == 0, SUBSTEPS * base_step, base_step)

    pl.when(fine_group & has_low)(lambda: far_copy(True).wait_recv())
    pl.when(fine_group & has_high)(lambda: far_copy(False).wait_recv())

    def step(i, carry):
        at = pl.multiple_of(HALO + i * wide_chunk, 8)
        advance(size, xa, xb, vel, vel, ext, mass, at, wide_chunk, frc[pl.ds(at, wide_chunk), :])
        return carry

    lax.fori_loop(0, wide_count, step, 0)
    size_out[...] = jnp.broadcast_to(size, size_out.shape)

    @pl.when(has_high)
    def _():
        for k in range(4):
            halo_copy(k, True).wait_send()

    @pl.when(has_low)
    def _():
        for k in range(4):
            halo_copy(k, False).wait_send()

    for j in range(3):
        guarded(exists[j], lambda j=j: trace_copy(j).wait_send())
    pl.when(fine_group & has_high)(lambda: far_copy(True).wait_send())
    pl.when(fine_group & has_low)(lambda: far_copy(False).wait_send())
    pltpu.make_async_copy(arrived, arrived, peak_send).wait()


def steps_kernel(
    xb, vel, ext, mass, thick, size_ref, band_hbm, disp_out, vel_out, xa, xc, held, band, load_sem, out_sem
):
    g = lax.axis_index("grp")
    rows = disp_out.shape[1]
    total = rows + 2 * BASE
    wide_chunk = row_chunk(rows + 2 * HALO, 352)
    wide_count = (rows + 2 * HALO) // wide_chunk
    plain_chunk = row_chunk(rows, 256)
    plain_count = rows // plain_chunk

    def outputs(src, vel, i):
        at = pl.multiple_of(i * plain_chunk, 8)
        here = pl.ds(BASE + at, plain_chunk)
        there = pl.ds(at, plain_chunk)
        return (
            pltpu.make_async_copy(src.at[here], disp_out.at[0, there], out_sem.at[0, i]),
            pltpu.make_async_copy(vel.at[here], vel_out.at[0, there], out_sem.at[1, i]),
        )

    def put(src, vel, i):
        for copy in outputs(src, vel, i):
            copy.start()

    def drain(src, vel):
        def step(i, carry):
            for copy in outputs(src, vel, i):
                copy.wait()
            return carry

        lax.fori_loop(0, plain_count, step, 0)

    @pl.when(g == 0)
    def _():
        for i in range(plain_count):
            put(xb, vel, i)
        drain(xb, vel)

    @pl.when(g == 1)
    def _():
        load = pltpu.make_async_copy(band_hbm, band, load_sem)
        load.start()
        size = size_ref[0:1, 0:1]
        zero = jnp.zeros((HALO, xa.shape[1]), jnp.float32)
        for buf in (xa, xc):
            buf[pl.ds(0, HALO), :] = zero
            buf[pl.ds(total - HALO, HALO), :] = zero
        load.wait()
        src, dst, speed = xb, xa, vel
        for _ in range(SUBSTEPS - 2):

            def step(i, carry, src=src, dst=dst, speed=speed):
                at = pl.multiple_of(HALO + i * wide_chunk, 8)
                inner = force(src, band, thick, at, wide_chunk)
                advance(size, src, dst, speed, held, ext, mass, at, wide_chunk, inner)
                return carry

            lax.fori_loop(0, wide_count, step, 0)
            src, dst, speed = dst, (xc if dst is xa else xa), held

        def last_step(i, carry):
            at = pl.multiple_of(BASE + i * plain_chunk, 8)
            inner = force(src, band, thick, at, plain_chunk)
            advance(size, src, dst, speed, held, ext, mass, at, plain_chunk, inner)
            put(dst, held, i)
            return carry

        lax.fori_loop(0, plain_count, last_step, 0)
        drain(dst, held)


def per_device(
    n_grp,
    n_patch,
    displace,
    velocity,
    ext_force,
    inv_mass,
    thickness,
    stiff_bands,
    pair_points,
    pair_weights,
):
    rows, width = displace.shape[1:]
    slots = pair_points.shape[3]
    total = rows + 2 * BASE
    blocks = rows // LANES
    points = pair_points.reshape(3, 1, slots)
    weights = pair_weights.reshape(3, 1, slots)
    bands = stiff_bands.reshape(stiff_bands.shape[0] * width, width)
    anywhere = pl.BlockSpec(memory_space=pl.ANY)
    vmem = pl.BlockSpec(memory_space=pltpu.VMEM)
    wide = pltpu.VMEM((total, width), jnp.float32)
    slim = pltpu.VMEM((total, POINTS), jnp.float32)
    dma = pltpu.SemaphoreType.DMA
    plain_count = rows // row_chunk(rows, 256)
    wide_out = pltpu.VMEM((total, width), jnp.float32)
    slim_out = pltpu.VMEM((total, POINTS), jnp.float32)
    state = pl.pallas_call(
        functools.partial(kernel, n_grp, n_patch),
        out_shape=[wide_out] * 3 + [slim_out] * 2 + [pltpu.VMEM((8, LANES), jnp.float32)],
        in_specs=[pl.BlockSpec(memory_space=pltpu.HBM)] * 6 + [vmem] * 2,
        out_specs=[vmem] * 6,
        scratch_shapes=[
            wide,
            wide,
            pltpu.VMEM(bands.shape, jnp.bfloat16),
            pltpu.VMEM((blocks * 16, LANES), jnp.bfloat16),
            pltpu.VMEM((3, 8, slots), jnp.float32),
            pltpu.VMEM((3, 8, slots), jnp.float32),
            pltpu.VMEM((blocks * 32, LANES), jnp.float32),
            pltpu.VMEM((n_grp * n_patch, 8, LANES), jnp.float32),
            dma((6,)),
            dma((4, 2)),
            dma((4, 2)),
            dma((3,)),
            dma((3,)),
            dma((2,)),
            dma((2,)),
            dma,
            dma,
        ],
        compiler_params=pltpu.CompilerParams(
            has_side_effects=True, vmem_limit_bytes=50 * 1024 * 1024
        ),
        name="couple_step",
    )(displace, velocity, ext_force, inv_mass, thickness, bands, points, weights)
    return pl.pallas_call(
        steps_kernel,
        out_shape=[jax.ShapeDtypeStruct(displace.shape, jnp.float32)] * 2,
        in_specs=[vmem] * 6 + [anywhere],
        out_specs=[anywhere] * 2,
        scratch_shapes=[
            wide,
            wide,
            wide,
            pltpu.VMEM(bands.shape, jnp.bfloat16),
            dma,
            dma((2, plain_count)),
        ],
        compiler_params=pltpu.CompilerParams(vmem_limit_bytes=24 * 1024 * 1024),
        name="fine_steps",
    )(*state, bands)


def solution(mesh):
    return jax.shard_map(
        functools.partial(per_device, mesh.shape["grp"], mesh.shape["patch"]),
        mesh=mesh,
        in_specs=(
            P("grp", "patch", None),
            P("grp", "patch", None),
            P("grp", "patch", None),
            P("grp", "patch", None),
            P("grp", "patch", None),
            P(),
            P("grp", "patch", None, None),
            P("grp", "patch", None, None),
        ),
        out_specs=(P("grp", "patch", None), P("grp", "patch", None)),
        check_vma=False,
    )
```
